512 devices in a mesh: row: 16 (over y, x), col: 32 (over z, core).
Axes of the slice: x: 4, y: 4, z: 16, core: 2. Of those that a mesh axis runs over, the one named last changes fastest.
Arguments:
- out_grad: bfloat16 [2048, 8192], P('col', 'row'), may hold values from -6 to 6
- hidden: bfloat16 [2048, 28672], P('row', 'col'), may hold values from -0.12988281 to 0.12988281
- weight: bfloat16 [28672, 8192], P('col', 'row'), may hold values from -0.03125 to 0.03125
Outputs:
- token_grad: bfloat16 [2048, 28672], P('row', 'col')
- weight_grad: bfloat16 [28672, 8192], P('col', 'row')
The draws below stay inside these ranges and needn't reach their ends.
All inputs are finite; a program needn't handle non-finite values.
Results may differ from the reference program's by a relative error of at most 0.001.
Values may be sent and summed in bfloat16 or wider, within the bound.
A program may use at most 64 MiB of HBM per device.

```python
import jax
import jax.numpy as jnp

D = 8192
FF = 28672
TOKENS = 2048


def spiked(array, stream_key, source, target, parts, factor):
    def block_of(axis_at):
        return (jnp.arange(array.shape[axis_at]) // (array.shape[axis_at] // parts)).reshape((-1,) + (1,) * (array.ndim - 1 - axis_at))

    near = jax.random.permutation(stream_key, parts)[block_of(target)]
    second = (block_of(target) + parts // 2) % parts
    return jnp.where((block_of(source) == near) | (block_of(source) == second), factor * array, array)


def level_of(own_key, shape, split, smallest, top_value):
    gain, own = 1.0, jax.random.fold_in(own_key, 6)
    for position, blocks in split:
        steps = jnp.exp(jax.random.uniform(jax.random.fold_in(own, position), (blocks,), jnp.float32, smallest / len(split), top_value / len(split)))
        gain = gain * jnp.repeat(steps, shape[position] // blocks).reshape([-1 if axis == position else 1 for axis in range(len(shape))])
    return gain


def bell_draw(key, shape, spread, bound, cuts=(), kind=jnp.bfloat16):
    drawn = spread * jax.random.normal(key, shape, jnp.float32)
    if cuts:
        drawn = drawn * level_of(key, shape, cuts, -0.22, 0.18)
    return jnp.clip(drawn, -bound, bound).astype(kind)


def gaussian_with(stream_key, extent, width, reach, split, heavy, dtype=jnp.bfloat16):
    drawn = width * jax.random.normal(stream_key, extent, jnp.float32)
    if split:
        drawn = drawn * level_of(stream_key, extent, split, -0.22, 0.18)
    return jnp.clip(spiked(drawn, jax.random.fold_in(stream_key, 3), *heavy), -reach, reach).astype(dtype)


def setup_inputs(seed: int = 0) -> dict:
    streams_of = jax.random.split(jax.random.key(seed), 4)
    return {
        "out_grad": gaussian_with(streams_of[0], (TOKENS, D), 1.0, 6.0, ((0, 32), (1, 16)), (1, 0, 32, 2.75)),
        "hidden": bell_draw(streams_of[1], (TOKENS, FF), 0.022, 0.12988281, ((0, 16), (1, 32))),
        "weight": bell_draw(streams_of[2], (FF, D), FF ** -0.5, 0.03125, ((0, 32), (1, 16))),
    }


def reference(out_grad, hidden, weight):
    token_grad = jnp.dot(out_grad, weight.T, preferred_element_type=jnp.float32).astype(jnp.bfloat16)
    weight_grad = jnp.dot(hidden.T, out_grad, preferred_element_type=jnp.float32).astype(jnp.bfloat16)
    return token_grad, weight_grad
```

```python
import jax
import jax.numpy as jnp
from jax import lax
from jax.experimental import pallas as pl
from jax.experimental.pallas import tpu as pltpu
from jax.sharding import PartitionSpec as P

MESH = pl.DeviceIdType.MESH
NX, NY, NZ = 4, 4, 16
BF16, F32 = jnp.bfloat16, jnp.float32
TOK = 64
WID = 512
PLANE = 2 * TOK
QUARTER = 256
HID = 896


def start_of(q):
    return pl.multiple_of(256 * q - 128 * lax.div(q, 3), 128)


def kernel(
    g_ref, h_ref, w_ref, tok_ref, wgt_ref,
    gf, wq, hq, pst, red, acc, wgs, wgo, tos, too,
    gp_s, gp_r, hx_s, hx_r, w_s, w_r, hy_s, hy_r,
    ring_s, ring_r, sib_s, sib_r, red_s, red_r, wo_s, wo_r, to_s, to_r,
):
    row, col = lax.axis_index("row"), lax.axis_index("col")
    x, y = lax.rem(row, NX), lax.div(row, NX)
    z, k = lax.div(col, 2), lax.rem(col, 2)

    def dev(x_, y_, z_, k_):
        return {"row": y_ * NX + x_, "col": z_ * 2 + k_}

    def xpeer(dx):
        return lax.rem(x + dx, NX)

    def ypeer(dy):
        return lax.rem(y + dy, NY)

    right, left = lax.rem(z + 1, NZ), lax.rem(z + NZ - 1, NZ)
    sibling = dev(x, y, z, 1 - k)

    def remote(src, dst, ss, rs, to):
        return pltpu.make_async_remote_copy(
            src_ref=src, dst_ref=dst, send_sem=ss, recv_sem=rs, device_id=to, device_id_type=MESH
        )

    barrier = pltpu.get_barrier_semaphore()
    partners = [dev(xpeer(d), y, z, k) for d in (1, 2, 3)]
    partners += [dev(x, ypeer(d), z, k) for d in (1, 2, 3)]
    partners += [dev(x, y, right, k), dev(x, y, left, k), sibling]
    for partner in partners:
        pl.semaphore_signal(barrier, inc=1, device_id=partner, device_id_type=MESH)
    pl.semaphore_wait(barrier, len(partners))

    def shard_at(d):
        return gf.at[
            lax.div(d, 2),
            pl.ds(pl.multiple_of(TOK * col, TOK), TOK),
            pl.ds(pl.multiple_of(WID * lax.rem(d, 2), WID), WID),
        ]

    def gp_copy(dx, owner):
        return remote(g_ref, shard_at(owner), gp_s.at[dx - 1], gp_r.at[dx - 1], dev(xpeer(dx), y, z, k))

    def hx_copy(dx, owner):
        to = xpeer(dx)
        return remote(
            h_ref.at[:, pl.ds(start_of(to), QUARTER)],
            hq.at[pl.ds(pl.multiple_of(PLANE * (NX * y + owner), PLANE), PLANE), :],
            hx_s.at[dx - 1], hx_r.at[dx - 1], dev(to, y, z, k),
        )

    def w_copy(dx, owner):
        to = xpeer(dx)
        return remote(
            w_ref.at[pl.ds(start_of(to), QUARTER), :], wq.at[owner],
            w_s.at[dx - 1], w_r.at[dx - 1], dev(to, y, z, k),
        )

    def hy_copy(dy, owner):
        rows = hq.at[pl.ds(pl.multiple_of(NX * PLANE * owner, NX * PLANE), NX * PLANE), :]
        return remote(rows, rows, hy_s.at[dy - 1], hy_r.at[dy - 1], dev(x, ypeer(dy), z, k))

    for dx in (1, 2, 3):
        gp_copy(dx, x).start()
    for dx in (1, 2, 3):
        hx_copy(dx, x).start()
    shard_at(x)[...] = g_ref[...]
    hq[pl.ds(pl.multiple_of(PLANE * row, PLANE), PLANE), :] = h_ref[:, pl.ds(start_of(x), QUARTER)]
    wq[x] = w_ref[pl.ds(start_of(x), QUARTER), :]

    def unit(p, core, h):
        return gf.at[h, pl.ds(pl.multiple_of(TOK * (2 * p + core), TOK), TOK), :]

    def away(direction, s):
        return lax.rem(z + NZ - s, NZ) if direction == 0 else lax.rem(z + s, NZ)

    def hop(direction, s, h):
        block = unit(away(direction, s - 1), k, h)
        to = right if direction == 0 else left
        return remote(block, block, ring_s.at[direction, s - 1, h], ring_r.at[direction, s - 1, h], dev(x, y, to, k))

    def landed(direction, s, h):
        block = unit(away(direction, s), k, h)
        remote(block, block, ring_s.at[direction, s - 1, h], ring_r.at[direction, s - 1, h], sibling).wait_recv()

    def across(p, h):
        block = unit(p, k, h)
        return remote(block, block, sib_s.at[p, h], sib_r.at[p, h], sibling)

    def crossed(p, h):
        block = unit(p, 1 - k, h)
        remote(block, block, sib_s.at[p, h], sib_r.at[p, h], sibling).wait_recv()

    for dx in (1, 2, 3):
        gp_copy(dx, xpeer(NX - dx)).wait_recv()
    for h in (0, 1):
        hop(0, 1, h).start()
        hop(1, 1, h).start()
        across(z, h).start()
    for dx in (1, 2, 3):
        w_copy(dx, x).start()
    for dx in (1, 2, 3):
        hx_copy(dx, xpeer(NX - dx)).wait_recv()
    for dy in (1, 2, 3):
        hy_copy(dy, y).start()

    acc[...] = jnp.zeros_like(acc)

    def service(s, h):
        for direction in (0, 1):
            landed(direction, s, h)
            if h == direction:
                hop(direction, s + 1, h).start()
            else:
                pl.when(s < 7)(lambda: hop(direction, s + 1, h).start())
            across(away(direction, s), h).start()

    def plane_of(n):
        return lax.rem(z + NZ + (1 - 2 * lax.rem(n, 2)) * lax.div(n + 1, 2), NZ)

    def red_copy(p):
        return remote(
            pst.at[p], red.at[y, lax.rem(p, NX)], red_s.at[p], red_r.at[y, lax.rem(p, NX)],
            dev(x, lax.div(p, NX), z, k),
        )

    def compute(n):
        p = plane_of(n)
        for h in (0, 1):
            crossed(p, h)
        rows = pl.ds(pl.multiple_of(PLANE * p, PLANE), PLANE)
        part = None
        for d in range(4):
            term = lax.dot_general(
                gf[d // 2, rows, WID * (d % 2):WID * (d % 2 + 1)], wq[d],
                (((1,), (1,)), ((), ())), preferred_element_type=F32,
            )
            part = term if part is None else part + term
        mine = lax.div(p, NX) == y

        @pl.when(mine)
        def _():
            red[y, lax.rem(p, NX)] = part

        @pl.when(jnp.logical_not(mine))
        def _():
            pst[p] = part
            red_copy(p).start()

        for d in range(4):
            acc[d] += lax.dot_general(
                hq[rows, :], gf[d // 2, rows, WID * (d % 2):WID * (d % 2 + 1)],
                (((0,), (0,)), ((), ())), preferred_element_type=F32,
            )

    def compute_range(lo, hi):
        lax.fori_loop(lo, hi, lambda n, c: (compute(n), c)[1], 0)

    def early(s, c):
        for h in (0, 1):
            service(s, h)
        return c

    lax.fori_loop(1, 3, early, 0)
    for dx in (1, 2, 3):
        w_copy(dx, xpeer(NX - dx)).wait_recv()
    for dy in (1, 2, 3):
        hy_copy(dy, ypeer(NY - dy)).wait_recv()

    def late(s, c):
        for h in (0, 1):
            service(s, h)
            t = 2 * (s - 3) + h
            compute_range(jnp.minimum(2 * t, 2 * s - 3 + h), jnp.minimum(2 * t + 2, 2 * s - 2 + h))
        return c

    lax.fori_loop(3, 8, late, 0)
    far = away(0, 8)
    for direction in (0, 1):
        landed(direction, 8, direction)
        across(far, direction).start()
    compute_range(13, 16)

    def wo_copy(dx, owner):
        to = xpeer(dx)
        return remote(wgs.at[to], wgo.at[owner], wo_s.at[dx - 1], wo_r.at[dx - 1], dev(to, y, z, k))

    def to_copy(dx, owner):
        to = xpeer(dx)
        return remote(tos.at[to], too.at[owner], to_s.at[dx - 1], to_r.at[dx - 1], dev(to, y, z, k))

    for d in range(4):
        wgs[d] = acc[d].astype(BF16)
    for dx in (1, 2, 3):
        wo_copy(dx, x).start()
    wgo[x] = wgs[x]

    for dx in (1, 2, 3, 0):
        xo = xpeer(dx)
        for dy in (1, 2, 3):
            src = ypeer(dy)
            remote(red.at[src, xo], red.at[src, xo], red_s.at[0], red_r.at[src, xo], sibling).wait_recv()
        tos[xo] = (red[0, xo] + red[1, xo] + red[2, xo] + red[3, xo]).astype(BF16)
        if dx:
            to_copy(dx, x).start()
        else:
            too[x] = tos[x]

    for dx in (1, 2, 3):
        to_copy(dx, xpeer(NX - dx)).wait_recv()
    for q in range(3):
        tok_ref[:, QUARTER * q:QUARTER * (q + 1)] = too[q]
    tok_ref[:, 768:] = too[3, :, 128:]
    for dx in (1, 2, 3):
        wo_copy(dx, xpeer(NX - dx)).wait_recv()
    for q in range(3):
        wgt_ref[QUARTER * q:QUARTER * (q + 1), :] = wgo[q]
    wgt_ref[768:, :] = wgo[3, 128:, :]

    for dx in (1, 2, 3):
        gp_copy(dx, x).wait_send()
        hx_copy(dx, x).wait_send()
        w_copy(dx, x).wait_send()
        hy_copy(dx, y).wait_send()
        wo_copy(dx, x).wait_send()
        to_copy(dx, x).wait_send()

    def drain(s, c):
        for h in (0, 1):
            hop(0, s, h).wait_send()
            hop(1, s, h).wait_send()
        return c

    lax.fori_loop(1, 8, drain, 0)
    hop(0, 8, 0).wait_send()
    hop(1, 8, 1).wait_send()

    def drain_planes(p, c):
        for h in (0, 1):
            across(p, h).wait_send()
        pl.when(lax.div(p, NX) != y)(lambda: red_copy(p).wait_send())
        return c

    lax.fori_loop(0, NZ, drain_planes, 0)


def on_device(out_grad, hidden, weight):
    dma = pltpu.SemaphoreType.DMA
    vmem = pl.BlockSpec(memory_space=pltpu.VMEM)
    return pl.pallas_call(
        kernel,
        out_shape=(
            jax.ShapeDtypeStruct((PLANE, HID), BF16),
            jax.ShapeDtypeStruct((HID, WID), BF16),
        ),
        in_specs=[vmem] * 3,
        out_specs=(vmem, vmem),
        scratch_shapes=[
            pltpu.VMEM((2, NZ * PLANE, 2 * WID), BF16),
            pltpu.VMEM((4, QUARTER, WID), BF16),
            pltpu.VMEM((NZ * PLANE, QUARTER), BF16),
            pltpu.VMEM((NZ, PLANE, QUARTER), F32),
            pltpu.VMEM((NY, NX, PLANE, QUARTER), F32),
            pltpu.VMEM((4, QUARTER, WID), F32),
            pltpu.VMEM((4, QUARTER, WID), BF16),
            pltpu.VMEM((4, QUARTER, WID), BF16),
            pltpu.VMEM((4, PLANE, QUARTER), BF16),
            pltpu.VMEM((4, PLANE, QUARTER), BF16),
            *[dma((3,))] * 8,
            dma((2, 8, 2)), dma((2, 8, 2)),
            dma((NZ, 2)), dma((NZ, 2)),
            dma((NZ,)), dma((NY, NX)),
            *[dma((3,))] * 4,
        ],
        compiler_params=pltpu.CompilerParams(
            collective_id=0, has_side_effects=True, vmem_limit_bytes=48 * 2**20
        ),
    )(out_grad, hidden, weight)


def solution(mesh):
    return jax.shard_map(
        on_device,
        mesh=mesh,
        in_specs=(P("col", "row"), P("row", "col"), P("col", "row")),
        out_specs=(P("row", "col"), P("col", "row")),
        check_vma=False,
    )
```

```python
import jax
import jax.numpy as jnp
from jax import lax
from jax.experimental import pallas as pl
from jax.experimental.pallas import tpu as pltpu
from jax.sharding import PartitionSpec as P

MESH = pl.DeviceIdType.MESH
NX, NY, NZ = 4, 4, 16
BF16, F32 = jnp.bfloat16, jnp.float32
TOK = 64
WID = 512
PLANE = 2 * TOK
QUARTER = 256
HID = 896
HEAD = 16
SLICE = 32
SPREAD, PER = 2, 2


def start_of(q):
    return pl.multiple_of(256 * q - 128 * lax.div(q, 3), 128)


def kernel(
    g_ref, h_ref, w_ref, tok_ref, wgt_ref,
    gf, wq, hf, pst, red, tos, too,
    own, gp_s, gp_r, a1_s, a1_r, b1_s, b1_r, w_s, w_r, a2_s, a2_r, b2_s, b2_r,
    ring_s, ring_r, sib_s, sib_r, red_s, red_r, to_s, to_r,
):
    row, col = lax.axis_index("row"), lax.axis_index("col")
    x, y = lax.rem(row, NX), lax.div(row, NX)
    z, k = lax.div(col, 2), lax.rem(col, 2)

    def dev(x_, y_, z_, k_):
        return {"row": y_ * NX + x_, "col": z_ * 2 + k_}

    def xpeer(dx):
        return lax.rem(x + dx, NX)

    def ypeer(dy):
        return lax.rem(y + dy, NY)

    right, left = lax.rem(z + 1, NZ), lax.rem(z + NZ - 1, NZ)
    sibling = dev(x, y, z, 1 - k)

    def rows(i, n):
        return pl.ds(pl.multiple_of(n * i, n), n)

    def remote(src, dst, ss, rs, to):
        return pltpu.make_async_remote_copy(
            src_ref=src, dst_ref=dst, send_sem=ss, recv_sem=rs, device_id=to, device_id_type=MESH
        )

    def head(p):
        return hf.at[pl.ds(pl.multiple_of(PLANE * p, PLANE), HEAD), :]

    def rest(p):
        return hf.at[pl.ds(pl.multiple_of(PLANE * p + HEAD, 16), PLANE - HEAD), :]

    locals_ = [
        pltpu.make_async_copy(g_ref, gf.at[x, rows(col, TOK), :], own.at[0]),
        pltpu.make_async_copy(w_ref.at[pl.ds(start_of(x), QUARTER), :], wq.at[x], own.at[1]),
        pltpu.make_async_copy(h_ref.at[pl.ds(0, HEAD), :], head(row), own.at[2]),
        pltpu.make_async_copy(h_ref.at[pl.ds(HEAD, PLANE - HEAD), :], rest(row), own.at[3]),
    ]
    for copy in locals_:
        copy.start()

    barrier = pltpu.get_barrier_semaphore()
    partners = [dev(x, y, right, k), dev(x, y, left, k), sibling]
    partners += [dev(xpeer(d), ypeer(e), z, k) for d in range(4) for e in range(4) if d or e]
    for partner in partners:
        pl.semaphore_signal(barrier, inc=1, device_id=partner, device_id_type=MESH)
    locals_[0].wait()
    pl.semaphore_wait(barrier, len(partners))

    def gp_copy(dx, owner):
        return remote(
            g_ref, gf.at[owner, rows(col, TOK), :], gp_s.at[dx - 1], gp_r.at[dx - 1], dev(xpeer(dx), y, z, k)
        )

    def w_copy(dx, owner):
        to = xpeer(dx)
        return remote(
            w_ref.at[pl.ds(start_of(to), QUARTER), :], wq.at[owner],
            w_s.at[dx - 1], w_r.at[dx - 1], dev(to, y, z, k),
        )

    def a1_copy(dx, owner):
        return remote(
            h_ref.at[pl.ds(0, HEAD), :], head(NX * y + owner),
            a1_s.at[dx - 1], a1_r.at[dx - 1], dev(xpeer(dx), y, z, k),
        )

    def a2_copy(dy, owner, i):
        block = head(NX * owner + i)
        return remote(block, block, a2_s.at[dy - 1, i], a2_r.at[dy - 1, i], dev(x, ypeer(dy), z, k))

    def b1_copy(dy, owner):
        return remote(
            h_ref.at[pl.ds(HEAD, PLANE - HEAD), :], rest(NX * owner + x),
            b1_s.at[dy - 1], b1_r.at[dy - 1], dev(x, ypeer(dy), z, k),
        )

    def b2_copy(dx, owner, i):
        block = rest(NX * i + owner)
        return remote(block, block, b2_s.at[dx - 1, i], b2_r.at[dx - 1, i], dev(xpeer(dx), y, z, k))

    def unit(p, core, j):
        return gf.at[xpeer(j), rows(2 * p + core, TOK), :]

    def away(direction, s):
        return lax.rem(z + NZ - s, NZ) if direction == 0 else lax.rem(z + s, NZ)

    def hop(direction, s, j):
        block = unit(away(direction, s - 1), k, j)
        to = right if direction == 0 else left
        return remote(block, block, ring_s.at[direction, s - 1, j], ring_r.at[direction, s - 1, j], dev(x, y, to, k))

    def landed(direction, s, j):
        block = unit(away(direction, s), k, j)
        remote(block, block, ring_s.at[direction, s - 1, j], ring_r.at[direction, s - 1, j], sibling).wait_recv()

    def across(p, j):
        block = unit(p, k, j)
        return remote(block, block, sib_s.at[p, j], sib_r.at[p, j], sibling)

    def crossed(p, j):
        block = unit(p, 1 - k, j)
        remote(block, block, sib_s.at[p, j], sib_r.at[p, j], sibling).wait_recv()

    for dx in (1, 2, 3):
        gp_copy(dx, x).start()
    for j in range(4):
        if j:
            gp_copy(NX - j, xpeer(j)).wait_recv()
        hop(0, 1, j).start()
        hop(1, 1, j).start()
        across(z, j).start()
        if j == 0:
            for d in (1, 2, 3):
                b1_copy(d, y).start()
    for d in (1, 2, 3):
        a1_copy(d, x).start()
    for d in (1, 2, 3):
        w_copy(d, x).start()

    def service(s, j):
        for direction in (0, 1):
            landed(direction, s, j)
            if j // 2 == direction:
                hop(direction, s + 1, j).start()
            elif s < 7:
                hop(direction, s + 1, j).start()
            across(away(direction, s), j).start()

    def plane_of(n):
        return lax.rem(z + NZ + (1 - 2 * lax.rem(n, 2)) * lax.div(n + 1, 2), NZ)

    def red_copy(p, dy):
        return remote(
            pst.at[p, rows(ypeer(dy), SLICE), :], red.at[dy - 1, p],
            red_s.at[p, dy - 1], red_r.at[p, dy - 1], dev(x, ypeer(dy), z, k),
        )

    def token_part(n):
        p = plane_of(n)
        for j in range(4):
            crossed(p, j)
        part = None
        for d in range(4):
            term = lax.dot_general(
                gf[d, rows(p, PLANE), :], wq[d], (((1,), (1,)), ((), ())), preferred_element_type=F32
            )
            part = term if part is None else part + term
        pst[p] = part
        for dy in (1, 2, 3):
            red_copy(p, dy).start()

    def to_copy(p, x_, y_):
        return remote(
            tos.at[p], too.at[x_, rows(y_, SLICE), :],
            to_s.at[p], to_r.at[x_, y_], dev(lax.rem(p, NX), lax.div(p, NX), z, k),
        )

    def finish(n):
        p = plane_of(n)
        for dy in (1, 2, 3):
            red_copy(p, dy).wait_recv()
        tos[p] = (pst[p, rows(y, SLICE), :] + red[0, p] + red[1, p] + red[2, p]).astype(BF16)

        @pl.when(p == row)
        def _():
            too[x, rows(y, SLICE), :] = tos[p]

        @pl.when(p != row)
        def _():
            to_copy(p, x, y).start()

    def weight_all():
        for d in (1, 2, 3):
            for i in range(4):
                a2_copy(d, ypeer(NY - d), i).wait_recv()
                b2_copy(d, xpeer(NX - d), i).wait_recv()
        for lo, hi in ((0, 256), (256, 512), (512, 768), (768, 896)):
            total = lax.dot_general(
                hf[:, lo:hi], gf[x], (((0,), (0,)), ((), ())), preferred_element_type=F32
            )
            wgt_ref[lo:hi, :] = total.astype(BF16)

    def each(part, lo, hi):
        lax.fori_loop(lo, hi, lambda n, c: (part(n), c)[1], 0)

    def step(s, *bodies):
        for j in range(4):
            service(s, j)
            for body in bodies:
                body(j)

    def spread(s):
        def body(j):
            m = 4 * (s - SPREAD) + j
            for i in range(PER * m, PER * (m + 1)):
                if i < 12:
                    a2_copy(i % 3 + 1, y, i // 3).start()
                    b2_copy(i % 3 + 1, x, i // 3).start()

        return body

    def plan(part, *ranges):
        def body(j):
            lo, hi = ranges[j]
            if hi > lo:
                each(part, lo, hi)

        return body

    none = (0, 0)
    step(1)
    for copy in locals_[2:]:
        copy.wait()
    for d in (1, 2, 3):
        b1_copy(d, ypeer(NY - d)).wait_recv()
        a1_copy(d, xpeer(NX - d)).wait_recv()
    step(2, spread(2))
    locals_[1].wait()
    for d in (1, 2, 3):
        w_copy(d, xpeer(NX - d)).wait_recv()
    step(3, spread(3), plan(token_part, (0, 1), (1, 2), (2, 3), (3, 4)))
    step(4, spread(4), plan(token_part, (4, 5), (5, 6), (6, 7), none))
    step(5, spread(5), plan(token_part, none, (7, 8), none, (8, 9)), plan(finish, (0, 3), none, (3, 5), none))
    step(6, spread(6), plan(token_part, none, (9, 10), none, (10, 11)), plan(finish, (5, 7), none, (7, 9), none))
    step(7, spread(7), plan(token_part, none, (11, 12), none, (12, 13)), plan(finish, (9, 10), none, (10, 11), none))
    far = away(0, 8)
    for direction in (0, 1):
        for j in (2 * direction, 2 * direction + 1):
            landed(direction, 8, j)
            across(far, j).start()
    each(token_part, 13, 15)
    each(token_part, 15, 16)
    each(finish, 11, 13)
    weight_all()
    each(finish, 13, 16)

    def arrived(i, c):
        pl.when(i != row)(lambda: to_copy(0, lax.rem(i, NX), lax.div(i, NX)).wait_recv())
        return c

    lax.fori_loop(0, NX * NY, arrived, 0)
    for q in range(3):
        tok_ref[:, QUARTER * q:QUARTER * (q + 1)] = too[q]
    tok_ref[:, 768:] = too[3, :, 128:]

    for d in (1, 2, 3):
        gp_copy(d, x).wait_send()
        w_copy(d, x).wait_send()
        a1_copy(d, x).wait_send()
        b1_copy(d, y).wait_send()
        for i in range(4):
            a2_copy(d, y, i).wait_send()
            b2_copy(d, x, i).wait_send()

    def drain(s, c):
        for j in range(4):
            hop(0, s, j).wait_send()
            hop(1, s, j).wait_send()
        return c

    lax.fori_loop(1, 8, drain, 0)
    for j in (0, 1):
        hop(0, 8, j).wait_send()
        hop(1, 8, 2 + j).wait_send()

    def drain_planes(p, c):
        for j in range(4):
            across(p, j).wait_send()
        for dy in (1, 2, 3):
            red_copy(p, dy).wait_send()
        pl.when(p != row)(lambda: to_copy(p, x, y).wait_send())
        return c

    lax.fori_loop(0, NZ, drain_planes, 0)


def on_device(out_grad, hidden, weight):
    dma = pltpu.SemaphoreType.DMA
    vmem = pl.BlockSpec(memory_space=pltpu.VMEM)
    return pl.pallas_call(
        kernel,
        out_shape=(
            jax.ShapeDtypeStruct((PLANE, HID), BF16),
            jax.ShapeDtypeStruct((HID, WID), BF16),
        ),
        in_specs=[pl.BlockSpec(memory_space=pl.ANY)] * 3,
        out_specs=(vmem, vmem),
        scratch_shapes=[
            pltpu.VMEM((4, NZ * PLANE, WID), BF16),
            pltpu.VMEM((4, QUARTER, WID), BF16),
            pltpu.VMEM((NZ * PLANE, HID), BF16),
            pltpu.VMEM((NZ, PLANE, QUARTER), F32),
            pltpu.VMEM((NY - 1, NZ, SLICE, QUARTER), F32),
            pltpu.VMEM((NZ, SLICE, QUARTER), BF16),
            pltpu.VMEM((4, PLANE, QUARTER), BF16),
            dma((4,)),
            *[dma((3,))] * 8,
            *[dma((3, 4))] * 4,
            dma((2, 8, 4)), dma((2, 8, 4)),
            dma((NZ, 4)), dma((NZ, 4)),
            dma((NZ, 3)), dma((NZ, 3)),
            dma((NZ,)), dma((NX, NY)),
        ],
        compiler_params=pltpu.CompilerParams(
            collective_id=0, has_side_effects=True, vmem_limit_bytes=48 * 2**20
        ),
    )(out_grad, hidden, weight)


def solution(mesh):
    return jax.shard_map(
        on_device,
        mesh=mesh,
        in_specs=(P("col", "row"), P("row", "col"), P("col", "row")),
        out_specs=(P("row", "col"), P("col", "row")),
        check_vma=False,
    )
```

```python
import jax
import jax.numpy as jnp
from jax import lax
from jax.experimental import pallas as pl
from jax.experimental.pallas import tpu as pltpu
from jax.sharding import PartitionSpec as P

MESH = pl.DeviceIdType.MESH
NX, NY, NZ = 4, 4, 16
BF16, F32 = jnp.bfloat16, jnp.float32
TOK = 64
WID = 512
PLANE = 2 * TOK
QUARTER = 256
HID = 896
HEAD = 16
SLICE = 32
SPREAD, PER = 2, 2


def start_of(q):
    return pl.multiple_of(256 * q - 128 * lax.div(q, 3), 128)


def kernel(
    g_ref, h_ref, w_ref, tok_ref, wgt_ref,
    gf, wq, hf, pst, red, tos, too,
    own, gp_s, gp_r, a1_s, a1_r, b1_s, b1_r, w_s, w_r, a2_s, a2_r, b2_s, b2_r,
    ring_s, ring_r, sib_s, sib_r, red_s, red_r, to_s, to_r,
):
    row, col = lax.axis_index("row"), lax.axis_index("col")
    x, y = lax.rem(row, NX), lax.div(row, NX)
    z, k = lax.div(col, 2), lax.rem(col, 2)

    def dev(x_, y_, z_, k_):
        return {"row": y_ * NX + x_, "col": z_ * 2 + k_}

    def xpeer(dx):
        return lax.rem(x + dx, NX)

    def ypeer(dy):
        return lax.rem(y + dy, NY)

    right, left = lax.rem(z + 1, NZ), lax.rem(z + NZ - 1, NZ)
    sibling = dev(x, y, z, 1 - k)

    def rows(i, n):
        return pl.ds(pl.multiple_of(n * i, n), n)

    def remote(src, dst, ss, rs, to):
        return pltpu.make_async_remote_copy(
            src_ref=src, dst_ref=dst, send_sem=ss, recv_sem=rs, device_id=to, device_id_type=MESH
        )

    def head(p):
        return hf.at[pl.ds(pl.multiple_of(PLANE * p, PLANE), HEAD), :]

    def rest(p):
        return hf.at[pl.ds(pl.multiple_of(PLANE * p + HEAD, 16), PLANE - HEAD), :]

    locals_ = [
        pltpu.make_async_copy(g_ref, gf.at[x, rows(col, TOK), :], own.at[0]),
        pltpu.make_async_copy(w_ref.at[pl.ds(start_of(x), QUARTER), :], wq.at[x], own.at[1]),
        pltpu.make_async_copy(h_ref.at[pl.ds(0, HEAD), :], head(row), own.at[2]),
        pltpu.make_async_copy(h_ref.at[pl.ds(HEAD, PLANE - HEAD), :], rest(row), own.at[3]),
    ]
    for copy in locals_:
        copy.start()

    barrier = pltpu.get_barrier_semaphore()
    partners = [dev(x, y, right, k), dev(x, y, left, k), sibling]
    partners += [dev(xpeer(d), ypeer(e), z, k) for d in range(4) for e in range(4) if d or e]
    for partner in partners:
        pl.semaphore_signal(barrier, inc=1, device_id=partner, device_id_type=MESH)
    locals_[0].wait()
    pl.semaphore_wait(barrier, len(partners))

    def gp_copy(dx, owner):
        return remote(
            g_ref, gf.at[owner, rows(col, TOK), :], gp_s.at[dx - 1], gp_r.at[dx - 1], dev(xpeer(dx), y, z, k)
        )

    def w_copy(dx, owner):
        to = xpeer(dx)
        return remote(
            w_ref.at[pl.ds(start_of(to), QUARTER), :], wq.at[owner],
            w_s.at[dx - 1], w_r.at[dx - 1], dev(to, y, z, k),
        )

    def a1_copy(dx, owner):
        return remote(
            h_ref.at[pl.ds(0, HEAD), :], head(NX * y + owner),
            a1_s.at[dx - 1], a1_r.at[dx - 1], dev(xpeer(dx), y, z, k),
        )

    def a2_copy(dy, owner, i):
        block = head(NX * owner + i)
        return remote(block, block, a2_s.at[dy - 1, i], a2_r.at[dy - 1, i], dev(x, ypeer(dy), z, k))

    def b1_copy(dy, owner):
        return remote(
            h_ref.at[pl.ds(HEAD, PLANE - HEAD), :], rest(NX * owner + x),
            b1_s.at[dy - 1], b1_r.at[dy - 1], dev(x, ypeer(dy), z, k),
        )

    def b2_copy(dx, owner, i):
        block = rest(NX * i + owner)
        return remote(block, block, b2_s.at[dx - 1, i], b2_r.at[dx - 1, i], dev(xpeer(dx), y, z, k))

    def unit(p, core, j):
        return gf.at[xpeer(j), rows(2 * p + core, TOK), :]

    def away(direction, s):
        return lax.rem(z + NZ - s, NZ) if direction == 0 else lax.rem(z + s, NZ)

    def hop(direction, s, j):
        block = unit(away(direction, s - 1), k, j)
        to = right if direction == 0 else left
        return remote(block, block, ring_s.at[direction, s - 1, j], ring_r.at[direction, s - 1, j], dev(x, y, to, k))

    def landed(direction, s, j):
        block = unit(away(direction, s), k, j)
        remote(block, block, ring_s.at[direction, s - 1, j], ring_r.at[direction, s - 1, j], sibling).wait_recv()

    def across(p, j):
        block = unit(p, k, j)
        return remote(block, block, sib_s.at[p, j], sib_r.at[p, j], sibling)

    def crossed(p, j):
        block = unit(p, 1 - k, j)
        remote(block, block, sib_s.at[p, j], sib_r.at[p, j], sibling).wait_recv()

    for dx in (1, 2, 3):
        gp_copy(dx, x).start()
    for j in range(4):
        if j:
            gp_copy(NX - j, xpeer(j)).wait_recv()
        hop(0, 1, j).start()
        hop(1, 1, j).start()
        across(z, j).start()
        if j == 0:
            for d in (1, 2, 3):
                b1_copy(d, y).start()
    for d in (1, 2, 3):
        a1_copy(d, x).start()
    for d in (1, 2, 3):
        w_copy(d, x).start()

    def service(s, j):
        for direction in (0, 1):
            landed(direction, s, j)
            if j // 2 == direction:
                hop(direction, s + 1, j).start()
            elif s < 7:
                hop(direction, s + 1, j).start()
            across(away(direction, s), j).start()

    def plane_of(n):
        return lax.rem(z + NZ + (1 - 2 * lax.rem(n, 2)) * lax.div(n + 1, 2), NZ)

    def red_copy(p, dy):
        return remote(
            pst.at[p, rows(ypeer(dy), SLICE), :], red.at[dy - 1, p],
            red_s.at[p, dy - 1], red_r.at[p, dy - 1], dev(x, ypeer(dy), z, k),
        )

    def token_part(n):
        p = plane_of(n)
        for j in range(4):
            crossed(p, j)
        part = None
        for d in range(4):
            term = lax.dot_general(
                gf[d, rows(p, PLANE), :], wq[d], (((1,), (1,)), ((), ())), preferred_element_type=F32
            )
            part = term if part is None else part + term
        pst[p] = part
        for dy in (1, 2, 3):
            red_copy(p, dy).start()

    def to_copy(p, x_, y_):
        return remote(
            tos.at[p], too.at[x_, rows(y_, SLICE), :],
            to_s.at[p], to_r.at[x_, y_], dev(lax.rem(p, NX), lax.div(p, NX), z, k),
        )

    def finish(n):
        p = plane_of(n)
        for dy in (1, 2, 3):
            red_copy(p, dy).wait_recv()
        tos[p] = (pst[p, rows(y, SLICE), :] + red[0, p] + red[1, p] + red[2, p]).astype(BF16)

        @pl.when(p == row)
        def _():
            too[x, rows(y, SLICE), :] = tos[p]

        @pl.when(p != row)
        def _():
            to_copy(p, x, y).start()

    def hidden_here():
        for d in (1, 2, 3):
            for i in range(4):
                a2_copy(d, ypeer(NY - d), i).wait_recv()
                b2_copy(d, xpeer(NX - d), i).wait_recv()
    def weight_part(*chunks):
        for lo, hi in chunks:
            total = lax.dot_general(
                hf[:, lo:hi], gf[x], (((0,), (0,)), ((), ())), preferred_element_type=F32
            )
            wgt_ref[lo:hi, :] = total.astype(BF16)

    def each(part, lo, hi):
        lax.fori_loop(lo, hi, lambda n, c: (part(n), c)[1], 0)

    def step(s, *bodies):
        for j in range(4):
            service(s, j)
            for body in bodies:
                body(j)

    def spread(s):
        def body(j):
            m = 4 * (s - SPREAD) + j
            for i in range(PER * m, PER * (m + 1)):
                if i < 12:
                    a2_copy(i % 3 + 1, y, i // 3).start()
                    b2_copy(i % 3 + 1, x, i // 3).start()

        return body

    def plan(part, *ranges):
        def body(j):
            lo, hi = ranges[j]
            if hi > lo:
                each(part, lo, hi)

        return body

    none = (0, 0)
    step(1)
    for copy in locals_[2:]:
        copy.wait()
    for d in (1, 2, 3):
        b1_copy(d, ypeer(NY - d)).wait_recv()
        a1_copy(d, xpeer(NX - d)).wait_recv()
    step(2, spread(2))
    step(3, spread(3))
    locals_[1].wait()
    for d in (1, 2, 3):
        w_copy(d, xpeer(NX - d)).wait_recv()
    step(4, plan(token_part, (0, 2), (2, 4), (4, 6), (6, 7)))
    step(5, spread(5), plan(token_part, none, (7, 8), none, (8, 9)), plan(finish, (0, 3), none, (3, 5), none))
    step(6, spread(6), plan(token_part, none, (9, 10), none, (10, 11)), plan(finish, (5, 7), none, (7, 9), none))
    step(7, spread(7), plan(token_part, none, (11, 12), none, (12, 13)), plan(finish, (9, 10), none, (10, 11), none))
    far = away(0, 8)
    for direction in (0, 1):
        for j in (2 * direction, 2 * direction + 1):
            landed(direction, 8, j)
            across(far, j).start()
    each(token_part, 13, 15)
    each(token_part, 15, 16)
    each(finish, 11, 13)
    hidden_here()
    weight_part((0, 256), (256, 512))
    each(finish, 13, 16)
    weight_part((512, 768), (768, 896))

    def arrived(i, c):
        pl.when(i != row)(lambda: to_copy(0, lax.rem(i, NX), lax.div(i, NX)).wait_recv())
        return c

    lax.fori_loop(0, NX * NY, arrived, 0)
    for q in range(3):
        tok_ref[:, QUARTER * q:QUARTER * (q + 1)] = too[q]
    tok_ref[:, 768:] = too[3, :, 128:]

    for d in (1, 2, 3):
        gp_copy(d, x).wait_send()
        w_copy(d, x).wait_send()
        a1_copy(d, x).wait_send()
        b1_copy(d, y).wait_send()
        for i in range(4):
            a2_copy(d, y, i).wait_send()
            b2_copy(d, x, i).wait_send()

    def drain(s, c):
        for j in range(4):
            hop(0, s, j).wait_send()
            hop(1, s, j).wait_send()
        return c

    lax.fori_loop(1, 8, drain, 0)
    for j in (0, 1):
        hop(0, 8, j).wait_send()
        hop(1, 8, 2 + j).wait_send()

    def drain_planes(p, c):
        for j in range(4):
            across(p, j).wait_send()
        for dy in (1, 2, 3):
            red_copy(p, dy).wait_send()
        pl.when(p != row)(lambda: to_copy(p, x, y).wait_send())
        return c

    lax.fori_loop(0, NZ, drain_planes, 0)


def on_device(out_grad, hidden, weight):
    dma = pltpu.SemaphoreType.DMA
    vmem = pl.BlockSpec(memory_space=pltpu.VMEM)
    return pl.pallas_call(
        kernel,
        out_shape=(
            jax.ShapeDtypeStruct((PLANE, HID), BF16),
            jax.ShapeDtypeStruct((HID, WID), BF16),
        ),
        in_specs=[pl.BlockSpec(memory_space=pltpu.HBM)] * 3,
        out_specs=(vmem, vmem),
        scratch_shapes=[
            pltpu.VMEM((4, NZ * PLANE, WID), BF16),
            pltpu.VMEM((4, QUARTER, WID), BF16),
            pltpu.VMEM((NZ * PLANE, HID), BF16),
            pltpu.VMEM((NZ, PLANE, QUARTER), F32),
            pltpu.VMEM((NY - 1, NZ, SLICE, QUARTER), F32),
            pltpu.VMEM((NZ, SLICE, QUARTER), BF16),
            pltpu.VMEM((4, PLANE, QUARTER), BF16),
            dma((4,)),
            *[dma((3,))] * 8,
            *[dma((3, 4))] * 4,
            dma((2, 8, 4)), dma((2, 8, 4)),
            dma((NZ, 4)), dma((NZ, 4)),
            dma((NZ, 3)), dma((NZ, 3)),
            dma((NZ,)), dma((NX, NY)),
        ],
        compiler_params=pltpu.CompilerParams(
            collective_id=0, has_side_effects=True, vmem_limit_bytes=53000 * 1024
        ),
    )(out_grad, hidden, weight)


def solution(mesh):
    return jax.shard_map(
        on_device,
        mesh=mesh,
        in_specs=(P("col", "row"), P("row", "col"), P("col", "row")),
        out_specs=(P("row", "col"), P("col", "row")),
        check_vma=False,
    )
```

```python
import jax
import jax.numpy as jnp
from jax import lax
from jax.experimental import pallas as pl
from jax.experimental.pallas import tpu as pltpu
from jax.sharding import PartitionSpec as P

MESH = pl.DeviceIdType.MESH
NX, NY, NZ = 4, 4, 16
BF16, F32 = jnp.bfloat16, jnp.float32
TOK = 64
WID = 512
PLANE = 2 * TOK
QUARTER = 256
HID = 896
HEAD = 16
SLICE = 32
SPREAD, PER = 2, 2


def start_of(q):
    return pl.multiple_of(256 * q - 128 * lax.div(q, 3), 128)


def kernel(
    g_ref, h_ref, w_ref, tok_ref, wgt_ref,
    gf, wq, hf, pst, red, tos, too,
    own, gp_s, gp_r, a1_s, a1_r, b1_s, b1_r, w_s, w_r, a2_s, a2_r, b2_s, b2_r,
    ring_s, ring_r, sib_s, sib_r, red_s, red_r, to_s, to_r,
):
    row, col = lax.axis_index("row"), lax.axis_index("col")
    x, y = lax.rem(row, NX), lax.div(row, NX)
    z, k = lax.div(col, 2), lax.rem(col, 2)

    def dev(x_, y_, z_, k_):
        return {"row": y_ * NX + x_, "col": z_ * 2 + k_}

    def xpeer(dx):
        return lax.rem(x + dx, NX)

    def ypeer(dy):
        return lax.rem(y + dy, NY)

    right, left = lax.rem(z + 1, NZ), lax.rem(z + NZ - 1, NZ)
    sibling = dev(x, y, z, 1 - k)

    def rows(i, n):
        return pl.ds(pl.multiple_of(n * i, n), n)

    def remote(src, dst, ss, rs, to):
        return pltpu.make_async_remote_copy(
            src_ref=src, dst_ref=dst, send_sem=ss, recv_sem=rs, device_id=to, device_id_type=MESH
        )

    def head(p):
        return hf.at[pl.ds(pl.multiple_of(PLANE * p, PLANE), HEAD), :]

    def rest(p):
        return hf.at[pl.ds(pl.multiple_of(PLANE * p + HEAD, 16), PLANE - HEAD), :]

    locals_ = [
        pltpu.make_async_copy(g_ref, gf.at[x, rows(col, TOK), :], own.at[0]),
        pltpu.make_async_copy(w_ref.at[pl.ds(start_of(x), QUARTER), :], wq.at[x], own.at[1]),
        pltpu.make_async_copy(h_ref.at[pl.ds(0, HEAD), :], head(row), own.at[2]),
        pltpu.make_async_copy(h_ref.at[pl.ds(HEAD, PLANE - HEAD), :], rest(row), own.at[3]),
    ]
    for copy in locals_:
        copy.start()

    barrier = pltpu.get_barrier_semaphore()
    partners = [dev(x, y, right, k), dev(x, y, left, k), sibling]
    partners += [dev(xpeer(d), ypeer(e), z, k) for d in range(4) for e in range(4) if d or e]
    for partner in partners:
        pl.semaphore_signal(barrier, inc=1, device_id=partner, device_id_type=MESH)
    locals_[0].wait()
    pl.semaphore_wait(barrier, len(partners))

    def gp_copy(dx, owner):
        return remote(
            g_ref, gf.at[owner, rows(col, TOK), :], gp_s.at[dx - 1], gp_r.at[dx - 1], dev(xpeer(dx), y, z, k)
        )

    def w_copy(dx, owner):
        to = xpeer(dx)
        return remote(
            w_ref.at[pl.ds(start_of(to), QUARTER), :], wq.at[owner],
            w_s.at[dx - 1], w_r.at[dx - 1], dev(to, y, z, k),
        )

    def a1_copy(dx, owner):
        return remote(
            h_ref.at[pl.ds(0, HEAD), :], head(NX * y + owner),
            a1_s.at[dx - 1], a1_r.at[dx - 1], dev(xpeer(dx), y, z, k),
        )

    def a2_copy(dy, owner, i):
        block = head(NX * owner + i)
        return remote(block, block, a2_s.at[dy - 1, i], a2_r.at[dy - 1, i], dev(x, ypeer(dy), z, k))

    def b1_copy(dy, owner):
        return remote(
            h_ref.at[pl.ds(HEAD, PLANE - HEAD), :], rest(NX * owner + x),
            b1_s.at[dy - 1], b1_r.at[dy - 1], dev(x, ypeer(dy), z, k),
        )

    def b2_copy(dx, owner, i):
        block = rest(NX * i + owner)
        return remote(block, block, b2_s.at[dx - 1, i], b2_r.at[dx - 1, i], dev(xpeer(dx), y, z, k))

    def unit(p, core, j):
        return gf.at[xpeer(j), rows(2 * p + core, TOK), :]

    def away(direction, s):
        return lax.rem(z + NZ - s, NZ) if direction == 0 else lax.rem(z + s, NZ)

    def hop(direction, s, j):
        block = unit(away(direction, s - 1), k, j)
        to = right if direction == 0 else left
        return remote(block, block, ring_s.at[direction, s - 1, j], ring_r.at[direction, s - 1, j], dev(x, y, to, k))

    def landed(direction, s, j):
        block = unit(away(direction, s), k, j)
        remote(block, block, ring_s.at[direction, s - 1, j], ring_r.at[direction, s - 1, j], sibling).wait_recv()

    def across(p, j):
        block = unit(p, k, j)
        return remote(block, block, sib_s.at[p, j], sib_r.at[p, j], sibling)

    def crossed(p, j):
        block = unit(p, 1 - k, j)
        remote(block, block, sib_s.at[p, j], sib_r.at[p, j], sibling).wait_recv()

    for dx in (1, 2, 3):
        gp_copy(dx, x).start()
    for j in range(4):
        if j:
            gp_copy(NX - j, xpeer(j)).wait_recv()
        hop(0, 1, j).start()
        hop(1, 1, j).start()
        across(z, j).start()
        if j == 0:
            for d in (1, 2, 3):
                b1_copy(d, y).start()
    for d in (1, 2, 3):
        a1_copy(d, x).start()
    for d in (1, 2, 3):
        w_copy(d, x).start()

    def service(s, j):
        for direction in (0, 1):
            landed(direction, s, j)
            if j // 2 == direction:
                hop(direction, s + 1, j).start()
            elif s < 7:
                hop(direction, s + 1, j).start()
            across(away(direction, s), j).start()

    def plane_of(n):
        return lax.rem(z + NZ + (1 - 2 * lax.rem(n, 2)) * lax.div(n + 1, 2), NZ)

    def red_copy(p, dy):
        return remote(
            pst.at[p, rows(ypeer(dy), SLICE), :], red.at[dy - 1, p],
            red_s.at[p, dy - 1], red_r.at[p, dy - 1], dev(x, ypeer(dy), z, k),
        )

    def token_part(n):
        p = plane_of(n)
        for j in range(4):
            crossed(p, j)
        part = None
        for d in range(4):
            term = lax.dot_general(
                gf[d, rows(p, PLANE), :], wq[d], (((1,), (1,)), ((), ())), preferred_element_type=F32
            )
            part = term if part is None else part + term
        pst[p] = part
        for dy in (1, 2, 3):
            red_copy(p, dy).start()

    def to_copy(p, x_, y_):
        return remote(
            tos.at[p], too.at[x_, rows(y_, SLICE), :],
            to_s.at[p], to_r.at[x_, y_], dev(lax.rem(p, NX), lax.div(p, NX), z, k),
        )

    def finish(n):
        p = plane_of(n)
        for dy in (1, 2, 3):
            red_copy(p, dy).wait_recv()
        tos[p] = (pst[p, rows(y, SLICE), :] + red[0, p] + red[1, p] + red[2, p]).astype(BF16)

        @pl.when(p == row)
        def _():
            too[x, rows(y, SLICE), :] = tos[p]

        @pl.when(p != row)
        def _():
            to_copy(p, x, y).start()

    def hidden_here():
        for d in (1, 2, 3):
            for i in range(4):
                a2_copy(d, ypeer(NY - d), i).wait_recv()
                b2_copy(d, xpeer(NX - d), i).wait_recv()
    def weight_part(*chunks):
        for lo, hi in chunks:
            total = lax.dot_general(
                hf[:, lo:hi], gf[x], (((0,), (0,)), ((), ())), preferred_element_type=F32
            )
            wgt_ref[lo:hi, :] = total.astype(BF16)

    def each(part, lo, hi):
        lax.fori_loop(lo, hi, lambda n, c: (part(n), c)[1], 0)

    def step(s, *bodies):
        for j in range(4):
            service(s, j)
            for body in bodies:
                body(j)

    def spread(s):
        def body(j):
            m = 4 * (s - SPREAD) + j
            for i in range(PER * m, PER * (m + 1)):
                if i < 12:
                    a2_copy(i % 3 + 1, y, i // 3).start()
                    b2_copy(i % 3 + 1, x, i // 3).start()

        return body

    def plan(part, *ranges):
        def body(j):
            lo, hi = ranges[j]
            if hi > lo:
                each(part, lo, hi)

        return body

    none = (0, 0)
    step(1)
    for copy in locals_[2:]:
        copy.wait()
    for d in (1, 2, 3):
        b1_copy(d, ypeer(NY - d)).wait_recv()
        a1_copy(d, xpeer(NX - d)).wait_recv()
    step(2, spread(2))
    step(3, spread(3))
    locals_[1].wait()
    for d in (1, 2, 3):
        w_copy(d, xpeer(NX - d)).wait_recv()
    step(4, plan(token_part, (0, 2), (2, 4), (4, 6), (6, 7)))
    step(5, spread(5), plan(token_part, none, (7, 8), none, (8, 9)), plan(finish, (0, 3), none, (3, 5), none))
    step(6, spread(6), plan(token_part, none, (9, 10), none, (10, 11)), plan(finish, (5, 7), none, (7, 9), none))
    step(7, spread(7), plan(token_part, none, (11, 12), none, (12, 13)), plan(finish, (9, 10), none, (10, 11), none))
    def drain_hops(s, c):
        for j in range(4):
            hop(0, s, j).wait_send()
            hop(1, s, j).wait_send()
        return c

    def sent(n):
        p = plane_of(n)
        for j in range(4):
            across(p, j).wait_send()
        for dy in (1, 2, 3):
            red_copy(p, dy).wait_send()

    def told(n):
        p = plane_of(n)
        pl.when(p != row)(lambda: to_copy(p, x, y).wait_send())

    far = away(0, 8)
    for direction in (0, 1):
        for j in (2 * direction, 2 * direction + 1):
            landed(direction, 8, j)
            across(far, j).start()
    each(token_part, 13, 15)
    each(token_part, 15, 16)
    each(finish, 11, 13)
    hidden_here()
    weight_part((0, 256), (256, 512))
    each(finish, 13, 16)
    weight_part((512, 768), (768, 896))
    for d in (1, 2, 3):
        gp_copy(d, x).wait_send()
        w_copy(d, x).wait_send()
        a1_copy(d, x).wait_send()
        b1_copy(d, y).wait_send()
        for i in range(4):
            a2_copy(d, y, i).wait_send()
            b2_copy(d, x, i).wait_send()
    lax.fori_loop(1, 7, drain_hops, 0)
    each(sent, 0, 11)
    each(told, 0, 9)
    lax.fori_loop(7, 8, drain_hops, 0)
    for j in (0, 1):
        hop(0, 8, j).wait_send()
        hop(1, 8, 2 + j).wait_send()
    each(sent, 11, 16)
    each(told, 9, 11)

    def arrived(i, c):
        pl.when(i != row)(lambda: to_copy(0, lax.rem(i, NX), lax.div(i, NX)).wait_recv())
        return c

    lax.fori_loop(0, NX * NY, arrived, 0)
    for q in range(3):
        tok_ref[:, QUARTER * q:QUARTER * (q + 1)] = too[q]
    tok_ref[:, 768:] = too[3, :, 128:]

    each(told, 11, 16)


def on_device(out_grad, hidden, weight):
    dma = pltpu.SemaphoreType.DMA
    vmem = pl.BlockSpec(memory_space=pltpu.VMEM)
    return pl.pallas_call(
        kernel,
        out_shape=(
            jax.ShapeDtypeStruct((PLANE, HID), BF16),
            jax.ShapeDtypeStruct((HID, WID), BF16),
        ),
        in_specs=[pl.BlockSpec(memory_space=pltpu.HBM)] * 3,
        out_specs=(vmem, vmem),
        scratch_shapes=[
            pltpu.VMEM((4, NZ * PLANE, WID), BF16),
            pltpu.VMEM((4, QUARTER, WID), BF16),
            pltpu.VMEM((NZ * PLANE, HID), BF16),
            pltpu.VMEM((NZ, PLANE, QUARTER), F32),
            pltpu.VMEM((NY - 1, NZ, SLICE, QUARTER), F32),
            pltpu.VMEM((NZ, SLICE, QUARTER), BF16),
            pltpu.VMEM((4, PLANE, QUARTER), BF16),
            dma((4,)),
            *[dma((3,))] * 8,
            *[dma((3, 4))] * 4,
            dma((2, 8, 4)), dma((2, 8, 4)),
            dma((NZ, 4)), dma((NZ, 4)),
            dma((NZ, 3)), dma((NZ, 3)),
            dma((NZ,)), dma((NX, NY)),
        ],
        compiler_params=pltpu.CompilerParams(
            collective_id=0, has_side_effects=True, vmem_limit_bytes=53000 * 1024
        ),
    )(out_grad, hidden, weight)


def solution(mesh):
    return jax.shard_map(
        on_device,
        mesh=mesh,
        in_specs=(P("col", "row"), P("row", "col"), P("col", "row")),
        out_specs=(P("row", "col"), P("col", "row")),
        check_vma=False,
    )
```
